32 devices in a mesh: ia: 4 (over z), ja: 4 (over x, core), ka: 2 (over y).
Axes of the slice: x: 2, y: 2, z: 4, core: 2. Of those that a mesh axis runs over, the one named last changes fastest.
Arguments:
- tensor: bfloat16 [64, 256, 512], P('ka', 'ia', 'ja'), may hold values from -768 to 768
- observed: int32 [64, 256, 512], P('ka', 'ia', 'ja'), may hold values from 0 to 1, as said below
- factor_a: bfloat16 [256, 128], P('ia', ('ja', 'ka')), may hold values from -6 to 6
- factor_b: bfloat16 [512, 128], P('ja', ('ia', 'ka')), may hold values from -6 to 6
- factor_c: bfloat16 [64, 128], P('ka', ('ia', 'ja')), may hold values from -6 to 6
Outputs:
- step_a: float32 [256, 128], P('ia', ('ja', 'ka'))
- step_b: float32 [512, 128], P('ja', ('ia', 'ka'))
- step_c: float32 [64, 128], P('ka', ('ia', 'ja'))
The draws below stay inside these ranges and needn't reach their ends.
Inputs may be any that keep to these rules, and one draw needn't show every extreme that they name: `observed`: a 0/1 weight per cell.
All inputs are finite; a program needn't handle non-finite values.
Results may differ from the reference program's by a relative error of at most 0.0095.
Values may be sent and summed in bfloat16 or wider, within the bound.
A program may use at most 64 MiB of HBM per device.

```python
import math
import jax
import jax.numpy as jnp
from jax import lax

RANK = 128
ITERS = 2
DIM_I = 256
DIM_J = 512
DIM_K = 64


def draw_observed(key, part):
    level_key = jax.random.fold_in(key, 11)
    cell_key = jax.random.fold_in(key, 23)
    blocks_k = (DIM_K + 3) // 4
    blocks_i = (DIM_I + 7) // 8
    blocks_j = (DIM_J + 31) // 32
    levels = jax.random.randint(level_key, (blocks_k, blocks_i, blocks_j), 0, 8)
    per_mille = jnp.array([10, 14, 19, 27, 37, 52, 72, 100], jnp.int32)
    limits = jnp.take(per_mille, levels)
    limits = jnp.broadcast_to(limits[:, None, :, None, :, None], (blocks_k, 4, blocks_i, 8, blocks_j, 32))
    limits = limits.reshape(blocks_k * 4, blocks_i * 8, blocks_j * 32)[:DIM_K, :DIM_I, :DIM_J]
    position = jnp.arange(DIM_I, dtype=jnp.int32)
    rising = (DIM_I + 9 * position)[None, :, None]
    limits = limits * rising // DIM_I
    chances = jax.random.randint(cell_key, (DIM_K, DIM_I, DIM_J), 0, 1000)
    return jnp.where(chances < limits, 1, 0).astype(jnp.int32)


def shard_levels(stream_key, extent, cuts, least, high):
    def one(dim, blocks):
        steps = jax.random.uniform(jax.random.fold_in(jax.random.fold_in(stream_key, 6), dim), (blocks,), jnp.float32, least / len(cuts), high / len(cuts))
        return jnp.repeat(jnp.exp(steps), extent[dim] // blocks).reshape((-1,) + (1,) * (len(extent) - dim - 1))

    gain = one(*cuts[0])
    for cut in cuts[1:]:
        gain = gain * one(*cut)
    return gain


def scatter_about(own_key, shape, scale, bound, pieces=(), held_as=jnp.bfloat16):
    entries = scale * jax.random.normal(own_key, shape, jnp.float32)
    if pieces:
        entries = entries * shard_levels(own_key, shape, pieces, -0.22, 0.18)
    return jnp.clip(entries, -bound, bound).astype(held_as)


def setup_inputs(seed: int = 0) -> dict:
    splits = jax.random.split(jax.random.key(seed), 6)
    tensor = scatter_about(splits[0], (DIM_K, DIM_I, DIM_J), 128.0, 768.0, ((0, 2), (1, 4), (2, 4)))
    observed = draw_observed(jax.random.fold_in(splits[5], 71), 0)
    factor_a = scatter_about(splits[2], (DIM_I, RANK), 1.0, 6.0, ((0, 4), (1, 8)))
    factor_b = scatter_about(splits[3], (DIM_J, RANK), 1.0, 6.0, ((0, 4), (1, 8)))
    factor_c = scatter_about(splits[4], (DIM_K, RANK), 1.0, 6.0, ((0, 2), (1, 16)))
    return {"tensor": tensor, "observed": observed, "factor_a": factor_a, "factor_b": factor_b, "factor_c": factor_c}


DAMP = 1.0


def against(left_side, right_side):
    return lax.dot_general(left_side, right_side, (((1,), (1,)), ((), ())), preferred_element_type=jnp.float32)


def reference(tensor, observed, factor_a, factor_b, factor_c):
    divisor = DIM_J * DIM_K / 32.0
    blocked = math.gcd(DIM_K, 8)
    count_blocks = DIM_K // blocked
    slabs = tensor.reshape(count_blocks, blocked, DIM_I, DIM_J)
    holes_all = observed.reshape(count_blocks, blocked, DIM_I, DIM_J)
    c_blocks = factor_c.reshape(count_blocks, blocked, RANK)
    wide_a = factor_a.astype(jnp.float32)

    def sweep(builder, extra):
        def advance(carry, inputs):
            slab, holes, c_block, hat_block = inputs
            wide_block = c_block.astype(jnp.float32)
            paired = (wide_block[:, None, :] * wide_a[None, :, :]).astype(jnp.bfloat16).reshape(blocked * DIM_I, RANK)
            weighted = builder(slab, holes, paired, wide_block, hat_block)
            part_b = lax.dot_general(weighted, paired, (((0,), (0,)), ((), ())), preferred_element_type=jnp.float32)
            mixture = jnp.dot(weighted, factor_b, preferred_element_type=jnp.float32).reshape(blocked, DIM_I, RANK)
            part_a = jnp.einsum("kir,kr->ir", mixture, wide_block)
            part_c = jnp.einsum("kir,ir->kr", mixture, wide_a)
            return (carry[0] + part_a, carry[1] + part_b), part_c

        start = (jnp.zeros((DIM_I, RANK), jnp.float32), jnp.zeros((DIM_J, RANK), jnp.float32))
        sums, parts_c = lax.scan(advance, start, (slabs, holes_all, c_blocks, extra))
        return sums[0], sums[1], parts_c.reshape(DIM_K, RANK)

    def residual_tile(slab, holes, paired, wide_block, hat_block):
        fitted = against(paired, factor_b)
        values = slab.reshape(-1, DIM_J).astype(jnp.float32)
        return (holes.reshape(-1, DIM_J).astype(jnp.float32) * (values - fitted) / divisor).astype(jnp.bfloat16)

    def hessian_times(direction):
        hat_a = direction[0].astype(jnp.bfloat16).astype(jnp.float32)
        hat_b = direction[1].astype(jnp.bfloat16)
        hat_c = direction[2].astype(jnp.bfloat16).reshape(count_blocks, blocked, RANK)

        def tangent_tile(slab, holes, paired, wide_block, hat_block):
            sideways = hat_block.astype(jnp.float32)[:, None, :] * wide_a[None, :, :] + wide_block[:, None, :] * hat_a[None, :, :]
            sideways = sideways.astype(jnp.bfloat16).reshape(blocked * DIM_I, RANK)
            tangent = against(paired, hat_b) + against(sideways, factor_b)
            return (holes.reshape(-1, DIM_J).astype(jnp.float32) * tangent / divisor).astype(jnp.bfloat16)

        parts = sweep(tangent_tile, hat_c)
        return tuple(part + DAMP * vector for part, vector in zip(parts, direction))

    def inner_sum(first, second):
        return sum(jnp.sum(left_side * right_side) for left_side, right_side in zip(first, second))

    gradient = sweep(residual_tile, c_blocks)
    solution = tuple(jnp.zeros_like(vector) for vector in gradient)
    residual = gradient
    direction = gradient
    norm_now = inner_sum(residual, residual)
    for iteration in range(ITERS):
        product = hessian_times(direction)
        step_size = norm_now / inner_sum(direction, product)
        solution = tuple(vector + step_size * update for vector, update in zip(solution, direction))
        if iteration + 1 < ITERS:
            residual = tuple(vector - step_size * update for vector, update in zip(residual, product))
            norm_next = inner_sum(residual, residual)
            direction = tuple(vector + (norm_next / norm_now) * update for vector, update in zip(residual, direction))
            norm_now = norm_next
    return solution[0], solution[1], solution[2]
```

```python
import functools

import jax
import jax.numpy as jnp
from jax import lax
from jax.experimental import pallas as pl
from jax.experimental.pallas import tpu as pltpu
from jax.sharding import PartitionSpec as P

DAMP = 1.0
CHUNK_K = 8
UNROLL = 40
F32 = jnp.float32
BF16 = jnp.bfloat16


def each(count, body):
    if count <= UNROLL:
        for step in range(1, count):
            body(step)
    else:
        lax.fori_loop(1, count, lambda step, carry: (body(step), carry)[1], 0)


def mm(left, right):
    return jnp.dot(left, right, preferred_element_type=F32)


def total(array):
    rows, cols = array.shape
    folded = jnp.sum(array.reshape(rows // 8, 8, cols), axis=0) if rows > 8 else array
    return jnp.sum(jnp.sum(folded, axis=0, keepdims=True), axis=1, keepdims=True)


def kernel(
    sizes,
    inverse,
    tensor_hbm,
    observed_hbm,
    fa_hbm,
    fb_hbm,
    fc_hbm,
    out_a,
    out_b,
    out_c,
    tensor,
    observed,
    slot_a,
    slot_b,
    slot_c,
    flip_a,
    flip_b,
    flip_c,
    paired,
    paired_t,
    first_t,
    send_a,
    send_b,
    send_c,
    recv_a,
    recv_b,
    recv_c,
    grad_a,
    grad_b,
    grad_c,
    send_s,
    recv_s,
    load_sem,
    gather_send,
    gather_recv,
    part_send,
    part_recv,
    scal_send,
    scal_recv,
):
    size_i, size_j, size_k = sizes
    ia, ja, ka = lax.axis_index("ia"), lax.axis_index("ja"), lax.axis_index("ka")
    count_a, count_b, count_c = size_j * size_k, size_i * size_k, size_i * size_j
    count = size_i * size_j * size_k
    rank_a, rank_b, rank_c = ja * size_k + ka, ia * size_k + ka, ia * size_j + ja
    rank = rank_c * size_k + ka

    def peer_a(step):
        other = lax.rem(rank_a + step, count_a)
        return (ia, lax.div(other, size_k), lax.rem(other, size_k))

    def peer_b(step):
        other = lax.rem(rank_b + step, count_b)
        return (lax.div(other, size_k), ja, lax.rem(other, size_k))

    def peer_c(step):
        other = lax.rem(rank_c + step, count_c)
        return (lax.div(other, size_j), lax.rem(other, size_j), ka)

    def peer_all(step):
        other = lax.rem(rank + step, count)
        pair = lax.div(other, size_k)
        return (lax.div(pair, size_j), lax.rem(pair, size_j), lax.rem(other, size_k))

    groups = ((count_a, peer_a), (count_b, peer_b), (count_c, peer_c))

    def send(source, target, send_sem, recv_sem, peer):
        pltpu.make_async_remote_copy(
            src_ref=source,
            dst_ref=target,
            send_sem=send_sem,
            recv_sem=recv_sem,
            device_id=peer,
            device_id_type=pl.DeviceIdType.MESH,
        ).start()

    def await_bytes(like, sem):
        pltpu.make_async_copy(like, like, sem).wait()

    load_tensor = pltpu.make_async_copy(tensor_hbm, tensor, load_sem.at[0])
    load_observed = pltpu.make_async_copy(observed_hbm, observed, load_sem.at[1])
    shards = ((fa_hbm, slot_a, rank_a), (fb_hbm, slot_b, rank_b), (fc_hbm, slot_c, rank_c))
    for index, (shard, slots, own) in enumerate(shards):
        pltpu.make_async_copy(shard, slots.at[own], gather_recv.at[index]).start()
    load_tensor.start()
    load_observed.start()

    barrier = pltpu.get_barrier_semaphore()

    def greet(step):
        pl.semaphore_signal(
            barrier, inc=1, device_id=peer_all(step), device_id_type=pl.DeviceIdType.MESH
        )

    each(count, greet)
    pl.semaphore_wait(barrier, count - 1)

    for index in (1, 0, 2):
        shard, slots, own = shards[index]
        members, peer = groups[index]

        def gather(step):
            send(shard, slots.at[own], gather_send.at[index], gather_recv.at[index], peer(step))

        each(members, gather)

    def assemble(index, slots, flip):
        await_bytes(slots, gather_recv.at[index])
        members, width, _ = slots.shape
        for step in range(members):
            flip[step * width : (step + 1) * width, :] = slots[step].astype(F32)
        return flip[...]

    wide_a = assemble(0, slot_a, flip_a).T
    wide_c = assemble(2, slot_c, flip_c).T
    turned_b = assemble(1, slot_b, flip_b)
    bt = turned_b.astype(BF16)
    full_b = turned_b.T.astype(BF16)
    depth, height, width = tensor.shape
    columns = wide_a.shape[1]
    rows = CHUNK_K * height
    chunks = depth // CHUNK_K
    load_tensor.wait()
    load_observed.wait()

    def weight_of(chunk):
        cells = observed[chunk * CHUNK_K : (chunk + 1) * CHUNK_K].reshape(rows, width)
        return cells.astype(F32) * inverse

    def pick(wide, chunk):
        return wide[chunk * CHUNK_K : (chunk + 1) * CHUNK_K][:, None, :]

    def spread(weighted, chunk, sums):
        mixture = mm(weighted, full_b).reshape(CHUNK_K, height, columns)
        sum_a = jnp.sum(mixture * pick(wide_c, chunk), axis=0)
        sum_c = jnp.sum(mixture * wide_a[None, :, :], axis=1)
        sum_b = mm(paired_t[:, chunk * rows : (chunk + 1) * rows], weighted)
        if sums is None:
            return [sum_a, sum_b, [sum_c]]
        return [sums[0] + sum_a, sums[1] + sum_b, sums[2] + [sum_c]]

    def fold(array):
        return jnp.sum(array.reshape(rows // 8, 8, width), axis=0)

    def share(turn, sums):
        own = (sums[0], sums[1], jnp.concatenate(sums[2], axis=0))
        for index, (outbox, inbox) in ((1, (send_b, recv_b)), (0, (send_a, recv_a)), (2, (send_c, recv_c))):
            outbox[turn] = own[index].astype(BF16)
            members, peer = groups[index]

            def post(step):
                send(
                    outbox.at[turn],
                    inbox.at[turn, step - 1],
                    part_send.at[turn, index],
                    part_recv.at[turn, index],
                    peer(step),
                )

            each(members, post)
        return own

    def collect(turn, index, own, inbox):
        await_bytes(inbox.at[turn], part_recv.at[turn, index])
        members = inbox.shape[1]
        if members <= UNROLL:
            result = own
            for step in range(members):
                result = result + inbox[turn, step].astype(F32)
            return result
        return lax.fori_loop(0, members, lambda step, acc: acc + inbox[turn, step].astype(F32), own)

    def share_scalars(turn, values):
        lane = lax.broadcasted_iota(jnp.int32, (1, 128), 1)
        row = jnp.zeros((1, 128), F32)
        for index, value in enumerate(values):
            row = jnp.where(lane == index, value, row)
        send_s[turn] = row

        def post(step):
            send(
                send_s.at[turn],
                recv_s.at[turn, step - 1],
                scal_send.at[turn],
                scal_recv.at[turn],
                peer_all(step),
            )

        each(count, post)
        return row

    def collect_scalars(turn, row, number):
        await_bytes(recv_s.at[turn], scal_recv.at[turn])
        row = row + jnp.sum(recv_s[turn], axis=0)
        return [row[:, index : index + 1] for index in range(number)]

    sums = None
    for chunk in range(chunks):
        span = slice(chunk * rows, (chunk + 1) * rows)
        pairs = (pick(wide_c, chunk) * wide_a[None, :, :]).reshape(rows, columns).astype(BF16)
        paired[span, :] = pairs
        paired_t[:, span] = pairs.T
        values = tensor[chunk * CHUNK_K : (chunk + 1) * CHUNK_K].reshape(rows, width).astype(F32)
        errors = (weight_of(chunk) * (values - mm(pairs, bt))).astype(BF16)
        sums = spread(errors, chunk, sums)
    own = share(0, sums)
    grad_b[...] = collect(0, 1, own[1], recv_b)
    grad_a[...] = collect(0, 0, own[0], recv_a)
    grad_c[...] = collect(0, 2, own[2], recv_c)

    shares = (1.0 / count_a, 1.0 / count_b, 1.0 / count_c)

    def inner(first, second):
        return sum(total(x * y) * part for x, y, part in zip(first, second, shares))

    def tangent_of(chunk, hat_a, hat_bt, hat_c):
        span = slice(chunk * rows, (chunk + 1) * rows)
        sideways = pick(hat_c, chunk) * wide_a[None, :, :] + pick(wide_c, chunk) * hat_a[None, :, :]
        sideways = sideways.reshape(rows, columns).astype(BF16)
        return mm(paired[span, :], hat_bt) + mm(sideways, bt)

    def rounded(triple):
        return (
            triple[0].astype(BF16).astype(F32),
            triple[1].astype(BF16),
            triple[2].astype(BF16).astype(F32),
        )

    gradient = (grad_a[...], grad_b[...], grad_c[...])
    hats = rounded(gradient)
    sums = None
    curve = jnp.zeros((8, width), F32)
    for chunk in range(chunks):
        tangent = tangent_of(chunk, *hats)
        first_t[chunk * rows : (chunk + 1) * rows, :] = tangent
        weighted = weight_of(chunk) * tangent
        curve = curve + fold(weighted * tangent)
        sums = spread(weighted.astype(BF16), chunk, sums)
    own = share(1, sums)
    row = share_scalars(0, (inner(gradient, gradient), total(curve)))
    gradient = (grad_a[...], grad_b[...], grad_c[...])
    product_b = collect(1, 1, own[1], recv_b) + DAMP * gradient[1]
    product_a = collect(1, 0, own[0], recv_a) + DAMP * gradient[0]
    product_c = collect(1, 2, own[2], recv_c) + DAMP * gradient[2]
    norm, curve_first = collect_scalars(0, row, 2)
    step_first = norm / (curve_first + DAMP * norm)
    residual = (
        gradient[0] - step_first * product_a,
        gradient[1] - step_first * product_b,
        gradient[2] - step_first * product_c,
    )

    hats = rounded(residual)
    curve = jnp.zeros((8, width), F32)
    cross = jnp.zeros((8, width), F32)
    for chunk in range(chunks):
        tangent = tangent_of(chunk, *hats)
        weighted = weight_of(chunk) * tangent
        curve = curve + fold(weighted * tangent)
        cross = cross + fold(weighted * first_t[chunk * rows : (chunk + 1) * rows, :])
    row = share_scalars(
        1, (inner(residual, residual), inner(residual, gradient), total(curve), total(cross))
    )

    def owned(flip, turned, own_rank, width_own):
        flip[...] = turned
        start = own_rank * width_own
        if width_own % 8 == 0:
            start = pl.multiple_of(start, 8)
        return flip[pl.ds(start, width_own), :]

    pieces = []
    for out, flip, own_rank, axis, turn in (
        (out_a, flip_a, rank_a, 0, True),
        (out_b, flip_b, rank_b, 1, False),
        (out_c, flip_c, rank_c, 2, True),
    ):
        width_own = out.shape[0]
        first = gradient[axis].T if turn else gradient[axis]
        second = residual[axis].T if turn else residual[axis]
        pieces.append(
            (out, owned(flip, first, own_rank, width_own), owned(flip, second, own_rank, width_own))
        )
    for sem_index, (like, members) in enumerate(
        ((slot_a, count_a), (slot_b, count_b), (slot_c, count_c))
    ):
        await_bytes(like.at[pl.ds(0, members - 1)], gather_send.at[sem_index])
    for turn in range(2):
        for index, inbox in enumerate((recv_a, recv_b, recv_c)):
            await_bytes(inbox.at[turn], part_send.at[turn, index])
        await_bytes(recv_s.at[turn], scal_send.at[turn])
    norm_next, mixed, curve_next, cross_next = collect_scalars(1, row, 4)
    ratio = norm_next / norm
    bottom = (
        curve_next
        + 2.0 * ratio * cross_next
        + ratio * ratio * curve_first
        + DAMP * (norm_next + 2.0 * ratio * mixed + ratio * ratio * norm)
    )
    step_second = norm_next / bottom
    along = step_first + step_second * ratio
    for out, first, second in pieces:
        out[...] = along * first + step_second * second


def local(tensor, observed, factor_a, factor_b, factor_c):
    sizes = (lax.axis_size("ia"), lax.axis_size("ja"), lax.axis_size("ka"))
    size_i, size_j, size_k = sizes
    count_a, count_b, count_c = size_j * size_k, size_i * size_k, size_i * size_j
    count = size_i * size_j * size_k
    depth, height, width = tensor.shape
    inverse = 32.0 / (width * size_j * depth * size_k)
    (own_a, own_b, own_c) = (factor_a.shape[1], factor_b.shape[1], factor_c.shape[1])
    columns = own_a * count_a
    cells = depth * height
    vmem = pltpu.VMEM
    outs = pl.pallas_call(
        functools.partial(kernel, sizes, inverse),
        out_shape=(
            jax.ShapeDtypeStruct((own_a, height), F32),
            jax.ShapeDtypeStruct((own_b, width), F32),
            jax.ShapeDtypeStruct((own_c, depth), F32),
        ),
        in_specs=[pl.BlockSpec(memory_space=pl.ANY)] * 5,
        out_specs=(pl.BlockSpec(memory_space=pltpu.VMEM),) * 3,
        scratch_shapes=[
            vmem((depth, height, width), tensor.dtype),
            vmem((depth, height, width), observed.dtype),
            vmem((count_a, own_a, height), BF16),
            vmem((count_b, own_b, width), BF16),
            vmem((count_c, own_c, depth), BF16),
            vmem((columns, height), F32),
            vmem((columns, width), F32),
            vmem((columns, depth), F32),
            vmem((cells, columns), BF16),
            vmem((columns, cells), BF16),
            vmem((cells, width), F32),
            vmem((2, height, columns), BF16),
            vmem((2, columns, width), BF16),
            vmem((2, depth, columns), BF16),
            vmem((2, count_a - 1, height, columns), BF16),
            vmem((2, count_b - 1, columns, width), BF16),
            vmem((2, count_c - 1, depth, columns), BF16),
            vmem((height, columns), F32),
            vmem((columns, width), F32),
            vmem((depth, columns), F32),
            vmem((2, 1, 128), F32),
            vmem((2, count - 1, 1, 128), F32),
            pltpu.SemaphoreType.DMA((2,)),
            pltpu.SemaphoreType.DMA((3,)),
            pltpu.SemaphoreType.DMA((3,)),
            pltpu.SemaphoreType.DMA((2, 3)),
            pltpu.SemaphoreType.DMA((2, 3)),
            pltpu.SemaphoreType.DMA((2,)),
            pltpu.SemaphoreType.DMA((2,)),
        ],
        compiler_params=pltpu.CompilerParams(collective_id=0, has_side_effects=True),
    )(tensor, observed, factor_a.T, factor_b.T, factor_c.T)
    return tuple(out.T for out in outs)


def solution(mesh):
    placed = (
        P("ka", "ia", "ja"),
        P("ka", "ia", "ja"),
        P("ia", ("ja", "ka")),
        P("ja", ("ia", "ka")),
        P("ka", ("ia", "ja")),
    )
    return jax.shard_map(
        local,
        mesh=mesh,
        in_specs=placed,
        out_specs=(P("ia", ("ja", "ka")), P("ja", ("ia", "ka")), P("ka", ("ia", "ja"))),
        check_vma=False,
    )
```

```python
import functools

import jax
import jax.numpy as jnp
from jax import lax
from jax.experimental import pallas as pl
from jax.experimental.pallas import tpu as pltpu
from jax.sharding import PartitionSpec as P

DAMP = 1.0
CHUNK_K = 8
UNROLL = 40
VMEM_LIMIT = 16 * 2**20
F32 = jnp.float32
BF16 = jnp.bfloat16


def each(count, body):
    if count <= UNROLL:
        for step in range(1, count):
            body(step)
    else:
        lax.fori_loop(1, count, lambda step, carry: (body(step), carry)[1], 0)


def mm(left, right):
    return jnp.dot(left, right, preferred_element_type=F32)


def total(array):
    rows, cols = array.shape
    folded = jnp.sum(array.reshape(rows // 8, 8, cols), axis=0) if rows > 8 else array
    return jnp.sum(jnp.sum(folded, axis=0, keepdims=True), axis=1, keepdims=True)


def kernel(
    sizes,
    inverse,
    tensor_hbm,
    observed_hbm,
    fa_hbm,
    fb_hbm,
    fc_hbm,
    out_a,
    out_b,
    out_c,
    tensor,
    observed,
    slot_a,
    slot_b,
    slot_c,
    flip_a,
    flip_b,
    flip_c,
    paired,
    paired_t,
    first_t,
    send_a,
    near_out_b,
    near_out_c,
    far_out_b,
    far_out_c,
    recv_a,
    near_b,
    near_c,
    far_b,
    far_c,
    grad_a,
    grad_b,
    grad_c,
    send_s,
    recv_s,
    load_sem,
    gather_send,
    gather_recv,
    part_send,
    part_recv,
    scal_send,
    scal_recv,
):
    size_i, size_j, size_k = sizes
    ia, ja, ka = lax.axis_index("ia"), lax.axis_index("ja"), lax.axis_index("ka")
    count_a, count_b, count_c = size_j * size_k, size_i * size_k, size_i * size_j
    count = size_i * size_j * size_k
    rank_a, rank_b, rank_c = ja * size_k + ka, ia * size_k + ka, ia * size_j + ja
    rank = rank_c * size_k + ka

    def peer_a(step):
        other = lax.rem(rank_a + step, count_a)
        return (ia, lax.div(other, size_k), lax.rem(other, size_k))

    def peer_b(step):
        other = lax.rem(rank_b + step, count_b)
        return (lax.div(other, size_k), ja, lax.rem(other, size_k))

    def peer_c(step):
        other = lax.rem(rank_c + step, count_c)
        return (lax.div(other, size_j), lax.rem(other, size_j), ka)

    def peer_all(step):
        other = lax.rem(rank + step, count)
        pair = lax.div(other, size_k)
        return (lax.div(pair, size_j), lax.rem(pair, size_j), lax.rem(other, size_k))

    def peer_i(step):
        return (lax.rem(ia + step, size_i), ja, ka)

    def peer_j(step):
        return (ia, lax.rem(ja + step, size_j), ka)

    def peer_k(step):
        return (ia, ja, lax.rem(ka + step, size_k))

    groups = ((count_a, peer_a), (count_b, peer_b), (count_c, peer_c))

    def send(source, target, send_sem, recv_sem, peer):
        pltpu.make_async_remote_copy(
            src_ref=source,
            dst_ref=target,
            send_sem=send_sem,
            recv_sem=recv_sem,
            device_id=peer,
            device_id_type=pl.DeviceIdType.MESH,
        ).start()

    def await_bytes(like, sem):
        pltpu.make_async_copy(like, like, sem).wait()

    load_tensor = pltpu.make_async_copy(tensor_hbm, tensor, load_sem.at[0])
    load_observed = pltpu.make_async_copy(observed_hbm, observed, load_sem.at[1])
    shards = ((fa_hbm, slot_a, rank_a), (fb_hbm, slot_b, rank_b), (fc_hbm, slot_c, rank_c))
    own_loads = [
        pltpu.make_async_copy(shard, slots.at[own], load_sem.at[2 + index])
        for index, (shard, slots, own) in enumerate(shards)
    ]
    for load in own_loads:
        load.start()
    load_tensor.start()
    load_observed.start()

    barrier = pltpu.get_barrier_semaphore()

    def greet(peer):
        pl.semaphore_signal(barrier, inc=1, device_id=peer, device_id_type=pl.DeviceIdType.MESH)

    for step_i in range(1, size_i):
        for step_j in range(1, size_j):
            greet((lax.rem(ia + step_i, size_i), lax.rem(ja + step_j, size_j), ka))
        for step_k in range(size_k):
            greet((lax.rem(ia + step_i, size_i), ja, lax.rem(ka + step_k, size_k)))
    each(count_a, lambda step: greet(peer_a(step)))
    for load in own_loads:
        load.wait()
    pl.semaphore_wait(barrier, (size_i - 1) * (size_j - 1 + size_k) + count_a - 1)

    for index in (1, 0, 2):
        _, slots, own = shards[index]
        members, peer = groups[index]

        def gather(step):
            send(slots.at[own], slots.at[own], gather_send.at[index], gather_recv.at[index], peer(step))

        each(members, gather)

    def assemble(index, slots, flip):
        members, width, _ = slots.shape
        await_bytes(slots.at[pl.ds(0, members - 1)], gather_recv.at[index])
        for step in range(members):
            flip[step * width : (step + 1) * width, :] = slots[step].astype(F32)
        return flip[...]

    wide_a = assemble(0, slot_a, flip_a).T
    wide_c = assemble(2, slot_c, flip_c).T
    turned_b = assemble(1, slot_b, flip_b)
    bt = turned_b.astype(BF16)
    full_b = turned_b.T.astype(BF16)
    depth, height, width = tensor.shape
    columns = wide_a.shape[1]
    rows = CHUNK_K * height
    chunks = depth // CHUNK_K
    load_tensor.wait()
    load_observed.wait()

    def weight_of(chunk):
        cells = observed[chunk * CHUNK_K : (chunk + 1) * CHUNK_K].reshape(rows, width)
        return cells.astype(F32) * inverse

    def pick(wide, chunk):
        return wide[chunk * CHUNK_K : (chunk + 1) * CHUNK_K][:, None, :]

    def spread(weighted, chunk, sums):
        mixture = mm(weighted, full_b).reshape(CHUNK_K, height, columns)
        sum_a = jnp.sum(mixture * pick(wide_c, chunk), axis=0)
        sum_c = jnp.sum(mixture * wide_a[None, :, :], axis=1)
        sum_b = mm(paired_t[:, chunk * rows : (chunk + 1) * rows], weighted)
        if sums is None:
            return [sum_a, sum_b, [sum_c]]
        return [sums[0] + sum_a, sums[1] + sum_b, sums[2] + [sum_c]]

    def fold(array):
        return jnp.sum(array.reshape(rows // 8, 8, width), axis=0)

    hops = (
        (send_a, recv_a, count_a, peer_a),
        (near_out_b, near_b, size_k, peer_k),
        (near_out_c, near_c, size_j, peer_j),
        (far_out_b, far_b, size_i, peer_i),
        (far_out_c, far_c, size_i, peer_i),
    )

    def post(turn, index, value):
        outbox, inbox, members, peer = hops[index]
        outbox[turn] = value.astype(BF16)

        def one(step):
            send(
                outbox.at[turn],
                inbox.at[turn, step - 1],
                part_send.at[turn, index],
                part_recv.at[turn, index],
                peer(step),
            )

        each(members, one)

    def collect(turn, index, own):
        inbox = hops[index][1]
        await_bytes(inbox.at[turn], part_recv.at[turn, index])
        for step in range(inbox.shape[1]):
            own = own + inbox[turn, step].astype(F32)
        return own

    def share(turn, sums):
        sum_a, sum_b, sum_c = sums[0], sums[1], jnp.concatenate(sums[2], axis=0)
        post(turn, 1, sum_b)
        post(turn, 2, sum_c)
        post(turn, 0, sum_a)
        return sum_a, sum_b, sum_c

    def settle(turn, own):
        sum_a, sum_b, sum_c = own
        sum_c = collect(turn, 2, sum_c)
        post(turn, 4, sum_c)
        sum_b = collect(turn, 1, sum_b)
        post(turn, 3, sum_b)
        sum_a = collect(turn, 0, sum_a)
        sum_c = collect(turn, 4, sum_c)
        sum_b = collect(turn, 3, sum_b)
        return sum_a, sum_b, sum_c

    def share_scalars(turn, values):
        lane = lax.broadcasted_iota(jnp.int32, (1, 128), 1)
        row = jnp.zeros((1, 128), F32)
        for index, value in enumerate(values):
            row = jnp.where(lane == index, value, row)
        send_s[turn] = row

        def post(step):
            send(
                send_s.at[turn],
                recv_s.at[turn, step - 1],
                scal_send.at[turn],
                scal_recv.at[turn],
                peer_all(step),
            )

        each(count, post)
        return row

    def collect_scalars(turn, row, number):
        await_bytes(recv_s.at[turn], scal_recv.at[turn])
        row = row + jnp.sum(recv_s[turn], axis=0)
        return [row[:, index : index + 1] for index in range(number)]

    sums = None
    for chunk in range(chunks):
        span = slice(chunk * rows, (chunk + 1) * rows)
        pairs = (pick(wide_c, chunk) * wide_a[None, :, :]).reshape(rows, columns).astype(BF16)
        paired[span, :] = pairs
        paired_t[:, span] = pairs.T
        values = tensor[chunk * CHUNK_K : (chunk + 1) * CHUNK_K].reshape(rows, width).astype(F32)
        errors = (weight_of(chunk) * (values - mm(pairs, bt))).astype(BF16)
        sums = spread(errors, chunk, sums)
    own = share(0, sums)
    grad_a[...], grad_b[...], grad_c[...] = settle(0, own)

    shares = (1.0 / count_a, 1.0 / count_b, 1.0 / count_c)

    def inner(first, second):
        return sum(total(x * y) * part for x, y, part in zip(first, second, shares))

    def tangent_of(chunk, hat_a, hat_bt, hat_c):
        span = slice(chunk * rows, (chunk + 1) * rows)
        sideways = pick(hat_c, chunk) * wide_a[None, :, :] + pick(wide_c, chunk) * hat_a[None, :, :]
        sideways = sideways.reshape(rows, columns).astype(BF16)
        return mm(paired[span, :], hat_bt) + mm(sideways, bt)

    def rounded(triple):
        return (
            triple[0].astype(BF16).astype(F32),
            triple[1].astype(BF16),
            triple[2].astype(BF16).astype(F32),
        )

    gradient = (grad_a[...], grad_b[...], grad_c[...])
    hats = rounded(gradient)
    sums = None
    curve = jnp.zeros((8, width), F32)
    for chunk in range(chunks):
        tangent = tangent_of(chunk, *hats)
        first_t[chunk * rows : (chunk + 1) * rows, :] = tangent
        weighted = weight_of(chunk) * tangent
        curve = curve + fold(weighted * tangent)
        sums = spread(weighted.astype(BF16), chunk, sums)
    own = share(1, sums)
    row = share_scalars(0, (inner(gradient, gradient), total(curve)))
    gradient = (grad_a[...], grad_b[...], grad_c[...])
    own = settle(1, own)
    product_a, product_b, product_c = (part + DAMP * p for part, p in zip(own, gradient))
    norm, curve_first = collect_scalars(0, row, 2)
    step_first = norm / (curve_first + DAMP * norm)
    residual = (
        gradient[0] - step_first * product_a,
        gradient[1] - step_first * product_b,
        gradient[2] - step_first * product_c,
    )

    hats = rounded(residual)
    curve = jnp.zeros((8, width), F32)
    cross = jnp.zeros((8, width), F32)
    for chunk in range(chunks):
        tangent = tangent_of(chunk, *hats)
        weighted = weight_of(chunk) * tangent
        curve = curve + fold(weighted * tangent)
        cross = cross + fold(weighted * first_t[chunk * rows : (chunk + 1) * rows, :])
    row = share_scalars(
        1, (inner(residual, residual), inner(residual, gradient), total(curve), total(cross))
    )

    def owned(flip, turned, own_rank, width_own):
        flip[...] = turned
        start = own_rank * width_own
        if width_own % 8 == 0:
            start = pl.multiple_of(start, 8)
        return flip[pl.ds(start, width_own), :]

    pieces = []
    for out, flip, own_rank, axis, turn in (
        (out_a, flip_a, rank_a, 0, True),
        (out_b, flip_b, rank_b, 1, False),
        (out_c, flip_c, rank_c, 2, True),
    ):
        width_own = out.shape[0]
        first = gradient[axis].T if turn else gradient[axis]
        second = residual[axis].T if turn else residual[axis]
        pieces.append(
            (out, owned(flip, first, own_rank, width_own), owned(flip, second, own_rank, width_own))
        )
    for sem_index, (like, members) in enumerate(
        ((slot_a, count_a), (slot_b, count_b), (slot_c, count_c))
    ):
        await_bytes(like.at[pl.ds(0, members - 1)], gather_send.at[sem_index])
    for turn in range(2):
        for index in range(5):
            await_bytes(hops[index][1].at[turn], part_send.at[turn, index])
        await_bytes(recv_s.at[turn], scal_send.at[turn])
    norm_next, mixed, curve_next, cross_next = collect_scalars(1, row, 4)
    ratio = norm_next / norm
    bottom = (
        curve_next
        + 2.0 * ratio * cross_next
        + ratio * ratio * curve_first
        + DAMP * (norm_next + 2.0 * ratio * mixed + ratio * ratio * norm)
    )
    step_second = norm_next / bottom
    along = step_first + step_second * ratio
    for out, first, second in pieces:
        out[...] = along * first + step_second * second


def hand_on(in_a, in_b, in_c, out_a, out_b, out_c, sems):
    copies = [
        pltpu.make_async_copy(source, target, sems.at[index])
        for index, (source, target) in enumerate(((in_a, out_a), (in_b, out_b), (in_c, out_c)))
    ]
    for copy in copies:
        copy.start()
    for copy in copies:
        copy.wait()


def local(tensor, observed, factor_a, factor_b, factor_c):
    sizes = (lax.axis_size("ia"), lax.axis_size("ja"), lax.axis_size("ka"))
    size_i, size_j, size_k = sizes
    count_a, count_b, count_c = size_j * size_k, size_i * size_k, size_i * size_j
    count = size_i * size_j * size_k
    depth, height, width = tensor.shape
    inverse = 32.0 / (width * size_j * depth * size_k)
    (own_a, own_b, own_c) = (factor_a.shape[1], factor_b.shape[1], factor_c.shape[1])
    columns = own_a * count_a
    cells = depth * height
    vmem = pltpu.VMEM
    operands = [
        pltpu.with_memory_space_constraint(operand, pltpu.HBM)
        for operand in (tensor, observed, factor_a.T, factor_b.T, factor_c.T)
    ]
    outs = pl.pallas_call(
        functools.partial(kernel, sizes, inverse),
        out_shape=(
            jax.ShapeDtypeStruct((own_a, height), F32),
            jax.ShapeDtypeStruct((own_b, width), F32),
            jax.ShapeDtypeStruct((own_c, depth), F32),
        ),
        in_specs=[pl.BlockSpec(memory_space=pltpu.HBM)] * 5,
        out_specs=(pl.BlockSpec(memory_space=pltpu.VMEM),) * 3,
        scratch_shapes=[
            vmem((depth, height, width), tensor.dtype),
            vmem((depth, height, width), observed.dtype),
            vmem((count_a, own_a, height), BF16),
            vmem((count_b, own_b, width), BF16),
            vmem((count_c, own_c, depth), BF16),
            vmem((columns, height), F32),
            vmem((columns, width), F32),
            vmem((columns, depth), F32),
            vmem((cells, columns), BF16),
            vmem((columns, cells), BF16),
            vmem((cells, width), F32),
            vmem((2, height, columns), BF16),
            vmem((2, columns, width), BF16),
            vmem((2, depth, columns), BF16),
            vmem((2, columns, width), BF16),
            vmem((2, depth, columns), BF16),
            vmem((2, count_a - 1, height, columns), BF16),
            vmem((2, size_k - 1, columns, width), BF16),
            vmem((2, size_j - 1, depth, columns), BF16),
            vmem((2, size_i - 1, columns, width), BF16),
            vmem((2, size_i - 1, depth, columns), BF16),
            vmem((height, columns), F32),
            vmem((columns, width), F32),
            vmem((depth, columns), F32),
            vmem((2, 1, 128), F32),
            vmem((2, count - 1, 1, 128), F32),
            pltpu.SemaphoreType.DMA((5,)),
            pltpu.SemaphoreType.DMA((3,)),
            pltpu.SemaphoreType.DMA((3,)),
            pltpu.SemaphoreType.DMA((2, 5)),
            pltpu.SemaphoreType.DMA((2, 5)),
            pltpu.SemaphoreType.DMA((2,)),
            pltpu.SemaphoreType.DMA((2,)),
        ],
        compiler_params=pltpu.CompilerParams(
            collective_id=0, has_side_effects=True, vmem_limit_bytes=VMEM_LIMIT
        ),
    )(*operands)
    outs = pl.pallas_call(
        hand_on,
        out_shape=tuple(jax.ShapeDtypeStruct(out.shape, F32) for out in outs),
        in_specs=[pl.BlockSpec(memory_space=pltpu.VMEM)] * 3,
        out_specs=(pl.BlockSpec(memory_space=pltpu.HBM),) * 3,
        scratch_shapes=[pltpu.SemaphoreType.DMA((3,))],
        compiler_params=pltpu.CompilerParams(vmem_limit_bytes=VMEM_LIMIT),
    )(*outs)
    return tuple(out.T for out in outs)


def solution(mesh):
    placed = (
        P("ka", "ia", "ja"),
        P("ka", "ia", "ja"),
        P("ia", ("ja", "ka")),
        P("ja", ("ia", "ka")),
        P("ka", ("ia", "ja")),
    )
    return jax.shard_map(
        local,
        mesh=mesh,
        in_specs=placed,
        out_specs=(P("ia", ("ja", "ka")), P("ja", ("ia", "ka")), P("ka", ("ia", "ja"))),
        check_vma=False,
    )
```

```python
import functools

import jax
import jax.numpy as jnp
from jax import lax
from jax.experimental import pallas as pl
from jax.experimental.pallas import tpu as pltpu
from jax.sharding import PartitionSpec as P

DAMP = 1.0
CHUNK_K = 8
UNROLL = 40
VMEM_LIMIT = 16 * 2**20
F32 = jnp.float32
BF16 = jnp.bfloat16


def each(count, body):
    if count <= UNROLL:
        for step in range(1, count):
            body(step)
    else:
        lax.fori_loop(1, count, lambda step, carry: (body(step), carry)[1], 0)


def mm(left, right):
    return jnp.dot(left, right, preferred_element_type=F32)


def total(array):
    rows, cols = array.shape
    folded = jnp.sum(array.reshape(rows // 8, 8, cols), axis=0) if rows > 8 else array
    return jnp.sum(jnp.sum(folded, axis=0, keepdims=True), axis=1, keepdims=True)


def kernel(
    sizes,
    inverse,
    tensor_hbm,
    observed_hbm,
    fa_hbm,
    fb_hbm,
    fc_hbm,
    out_a,
    out_b,
    out_c,
    tensor,
    observed,
    slot_a,
    slot_b,
    slot_c,
    flip_a,
    flip_b,
    flip_c,
    paired,
    paired_t,
    first_t,
    second_t,
    send_a,
    near_out_b,
    near_out_c,
    far_out_b,
    far_out_c,
    recv_a,
    near_b,
    near_c,
    far_b,
    far_c,
    grad_a,
    grad_b,
    grad_c,
    send_s,
    recv_s,
    load_sem,
    gather_send,
    gather_recv,
    part_send,
    part_recv,
    scal_send,
    scal_recv,
):
    size_i, size_j, size_k = sizes
    ia, ja, ka = lax.axis_index("ia"), lax.axis_index("ja"), lax.axis_index("ka")
    count_a, count_b, count_c = size_j * size_k, size_i * size_k, size_i * size_j
    count = size_i * size_j * size_k
    rank_a, rank_b, rank_c = ja * size_k + ka, ia * size_k + ka, ia * size_j + ja
    rank = rank_c * size_k + ka

    def peer_a(step):
        other = lax.rem(rank_a + step, count_a)
        return (ia, lax.div(other, size_k), lax.rem(other, size_k))

    def peer_b(step):
        other = lax.rem(rank_b + step, count_b)
        return (lax.div(other, size_k), ja, lax.rem(other, size_k))

    def peer_c(step):
        other = lax.rem(rank_c + step, count_c)
        return (lax.div(other, size_j), lax.rem(other, size_j), ka)

    def peer_all(step):
        other = lax.rem(rank + step, count)
        pair = lax.div(other, size_k)
        return (lax.div(pair, size_j), lax.rem(pair, size_j), lax.rem(other, size_k))

    def peer_i(step):
        return (lax.rem(ia + step, size_i), ja, ka)

    def peer_j(step):
        return (ia, lax.rem(ja + step, size_j), ka)

    def peer_k(step):
        return (ia, ja, lax.rem(ka + step, size_k))

    groups = ((count_a, peer_a), (count_b, peer_b), (count_c, peer_c))

    def send(source, target, send_sem, recv_sem, peer):
        pltpu.make_async_remote_copy(
            src_ref=source,
            dst_ref=target,
            send_sem=send_sem,
            recv_sem=recv_sem,
            device_id=peer,
            device_id_type=pl.DeviceIdType.MESH,
        ).start()

    def await_bytes(like, sem):
        pltpu.make_async_copy(like, like, sem).wait()

    barrier = pltpu.get_barrier_semaphore()

    def greet(peer):
        pl.semaphore_signal(barrier, inc=1, device_id=peer, device_id_type=pl.DeviceIdType.MESH)

    for step_i in range(1, size_i):
        for step_j in range(1, size_j):
            greet((lax.rem(ia + step_i, size_i), lax.rem(ja + step_j, size_j), ka))
        for step_k in range(size_k):
            greet((lax.rem(ia + step_i, size_i), ja, lax.rem(ka + step_k, size_k)))
    each(count_a, lambda step: greet(peer_a(step)))
    load_tensor = pltpu.make_async_copy(tensor_hbm, tensor, load_sem.at[0])
    load_observed = pltpu.make_async_copy(observed_hbm, observed, load_sem.at[1])
    shards = ((fa_hbm, slot_a, rank_a), (fb_hbm, slot_b, rank_b), (fc_hbm, slot_c, rank_c))
    own_loads = [
        pltpu.make_async_copy(shard, slots.at[own], load_sem.at[2 + index])
        for index, (shard, slots, own) in enumerate(shards)
    ]
    for load in own_loads:
        load.start()
    load_tensor.start()
    load_observed.start()

    for load in own_loads:
        load.wait()
    pl.semaphore_wait(barrier, (size_i - 1) * (size_j - 1 + size_k) + count_a - 1)

    for index in (2, 0, 1):
        _, slots, own = shards[index]
        members, peer = groups[index]

        def gather(step):
            send(slots.at[own], slots.at[own], gather_send.at[index], gather_recv.at[index], peer(step))

        each(members, gather)

    def assemble(index, slots, flip):
        members, width, _ = slots.shape
        await_bytes(slots.at[pl.ds(0, members - 1)], gather_recv.at[index])
        for step in range(members):
            flip[step * width : (step + 1) * width, :] = slots[step].astype(F32)
        return flip[...]

    wide_a = assemble(0, slot_a, flip_a).T
    wide_c = assemble(2, slot_c, flip_c).T
    depth, height, width = tensor.shape
    columns = wide_a.shape[1]
    rows = CHUNK_K * height
    chunks = depth // CHUNK_K

    def weight_of(chunk):
        cells = observed[chunk * CHUNK_K : (chunk + 1) * CHUNK_K].reshape(rows, width)
        return cells.astype(F32) * inverse

    def pick(wide, chunk):
        return wide[chunk * CHUNK_K : (chunk + 1) * CHUNK_K][:, None, :]

    for chunk in range(chunks):
        span = slice(chunk * rows, (chunk + 1) * rows)
        pairs = (pick(wide_c, chunk) * wide_a[None, :, :]).reshape(rows, columns).astype(BF16)
        paired[span, :] = pairs
        paired_t[:, span] = pairs.T
    turned_b = assemble(1, slot_b, flip_b)
    bt = turned_b.astype(BF16)
    full_b = turned_b.T.astype(BF16)
    load_tensor.wait()
    load_observed.wait()

    def spread(weighted, chunk, sums):
        mixture = mm(weighted, full_b).reshape(CHUNK_K, height, columns)
        sum_a = jnp.sum(mixture * pick(wide_c, chunk), axis=0)
        sum_c = jnp.sum(mixture * wide_a[None, :, :], axis=1)
        sum_b = mm(paired_t[:, chunk * rows : (chunk + 1) * rows], weighted)
        if sums is None:
            return [sum_a, sum_b, [sum_c]]
        return [sums[0] + sum_a, sums[1] + sum_b, sums[2] + [sum_c]]

    def fold(array):
        return jnp.sum(array.reshape(rows // 8, 8, width), axis=0)

    hops = (
        (send_a, recv_a, count_a, peer_a),
        (near_out_b, near_b, size_k, peer_k),
        (near_out_c, near_c, size_j, peer_j),
        (far_out_b, far_b, size_i, peer_i),
        (far_out_c, far_c, size_i, peer_i),
    )

    def post(turn, index, value):
        outbox, inbox, members, peer = hops[index]
        outbox[turn] = value.astype(BF16)

        def one(step):
            send(
                outbox.at[turn],
                inbox.at[turn, step - 1],
                part_send.at[turn, index],
                part_recv.at[turn, index],
                peer(step),
            )

        each(members, one)

    def collect(turn, index, own):
        inbox = hops[index][1]
        await_bytes(inbox.at[turn], part_recv.at[turn, index])
        for step in range(inbox.shape[1]):
            own = own + inbox[turn, step].astype(F32)
        return own

    def share(turn, sums):
        sum_a, sum_b, sum_c = sums[0], sums[1], jnp.concatenate(sums[2], axis=0)
        post(turn, 1, sum_b)
        post(turn, 2, sum_c)
        return sum_a, sum_b, sum_c

    def settle_ac(turn, own):
        sum_a, sum_b, sum_c = own
        sum_c = collect(turn, 2, sum_c)
        post(turn, 4, sum_c)
        sum_b = collect(turn, 1, sum_b)
        post(turn, 3, sum_b)
        post(turn, 0, sum_a)
        sum_a = collect(turn, 0, sum_a)
        sum_c = collect(turn, 4, sum_c)
        return sum_a, sum_b, sum_c

    def share_scalars(turn, values):
        lane = lax.broadcasted_iota(jnp.int32, (1, 128), 1)
        row = jnp.zeros((1, 128), F32)
        for index, value in enumerate(values):
            row = jnp.where(lane == index, value, row)
        send_s[turn] = row

        def post(step):
            send(
                send_s.at[turn],
                recv_s.at[turn, step - 1],
                scal_send.at[turn],
                scal_recv.at[turn],
                peer_all(step),
            )

        each(count, post)
        return row

    def collect_scalars(turn, row, number):
        await_bytes(recv_s.at[turn], scal_recv.at[turn])
        row = row + jnp.sum(recv_s[turn], axis=0)
        return [row[:, index : index + 1] for index in range(number)]

    sums = None
    for chunk in range(chunks):
        span = slice(chunk * rows, (chunk + 1) * rows)
        values = tensor[chunk * CHUNK_K : (chunk + 1) * CHUNK_K].reshape(rows, width).astype(F32)
        errors = (weight_of(chunk) * (values - mm(paired[span, :], bt))).astype(BF16)
        sums = spread(errors, chunk, sums)
    own = share(0, sums)
    shares = (1.0 / count_a, 1.0 / count_b, 1.0 / count_c)

    def inner(first, second, axes):
        return sum(total(first[axis] * second[axis]) * shares[axis] for axis in axes)

    def span_of(chunk):
        return slice(chunk * rows, (chunk + 1) * rows)

    def sideways_of(result, hat_a, hat_c):
        for chunk in range(chunks):
            mixed_a = pick(hat_c, chunk) * wide_a[None, :, :]
            mixed_c = pick(wide_c, chunk) * hat_a[None, :, :]
            result[span_of(chunk), :] = mm((mixed_a + mixed_c).reshape(rows, columns).astype(BF16), bt)

    def wide_hat(array):
        return array.astype(BF16).astype(F32)

    sum_a, sum_b, sum_c = settle_ac(0, own)
    grad_a[...] = sum_a
    grad_c[...] = sum_c
    sideways_of(first_t, wide_hat(sum_a), wide_hat(sum_c))
    sum_b = collect(0, 3, sum_b)
    grad_b[...] = sum_b

    hat_b = sum_b.astype(BF16)
    sums = None
    curve = jnp.zeros((8, width), F32)
    for chunk in range(chunks):
        tangent = first_t[span_of(chunk), :] + mm(paired[span_of(chunk), :], hat_b)
        first_t[span_of(chunk), :] = tangent
        weighted = weight_of(chunk) * tangent
        curve = curve + fold(weighted * tangent)
        sums = spread(weighted.astype(BF16), chunk, sums)
    own = share(1, sums)
    gradient = (grad_a[...], grad_b[...], grad_c[...])
    row = share_scalars(0, (inner(gradient, gradient, (0, 1, 2)), total(curve)))
    sum_a, sum_b, sum_c = settle_ac(1, own)
    norm, curve_first = collect_scalars(0, row, 2)
    step_first = norm / (curve_first + DAMP * norm)
    gradient = (grad_a[...], grad_b[...], grad_c[...])

    def residual_of(axis, part):
        return gradient[axis] - step_first * (part + DAMP * gradient[axis])

    rest_a, rest_c = residual_of(0, sum_a), residual_of(2, sum_c)
    sideways_of(second_t, wide_hat(rest_a), wide_hat(rest_c))
    residual = (rest_a, None, rest_c)
    norm_next = inner(residual, residual, (0, 2))
    mixed = inner(residual, gradient, (0, 2))
    residual = (rest_a, residual_of(1, collect(1, 3, sum_b)), rest_c)

    hat_b = residual[1].astype(BF16)
    curve = jnp.zeros((8, width), F32)
    cross = jnp.zeros((8, width), F32)
    for chunk in range(chunks):
        tangent = second_t[span_of(chunk), :] + mm(paired[span_of(chunk), :], hat_b)
        weighted = weight_of(chunk) * tangent
        curve = curve + fold(weighted * tangent)
        cross = cross + fold(weighted * first_t[span_of(chunk), :])
    norm_next = norm_next + inner(residual, residual, (1,))
    mixed = mixed + inner(residual, gradient, (1,))
    row = share_scalars(1, (norm_next, mixed, total(curve), total(cross)))

    def owned(flip, turned, own_rank, width_own):
        flip[...] = turned
        start = own_rank * width_own
        if width_own % 8 == 0:
            start = pl.multiple_of(start, 8)
        return flip[pl.ds(start, width_own), :]

    pieces = []
    for out, flip, own_rank, axis, turn in (
        (out_a, flip_a, rank_a, 0, True),
        (out_b, flip_b, rank_b, 1, False),
        (out_c, flip_c, rank_c, 2, True),
    ):
        width_own = out.shape[0]
        first = gradient[axis].T if turn else gradient[axis]
        second = residual[axis].T if turn else residual[axis]
        pieces.append(
            (out, owned(flip, first, own_rank, width_own), owned(flip, second, own_rank, width_own))
        )
    for sem_index, (like, members) in enumerate(
        ((slot_a, count_a), (slot_b, count_b), (slot_c, count_c))
    ):
        await_bytes(like.at[pl.ds(0, members - 1)], gather_send.at[sem_index])
    for turn in range(2):
        for index in range(5):
            await_bytes(hops[index][1].at[turn], part_send.at[turn, index])
        await_bytes(recv_s.at[turn], scal_send.at[turn])
    norm_next, mixed, curve_next, cross_next = collect_scalars(1, row, 4)
    ratio = norm_next / norm
    bottom = (
        curve_next
        + 2.0 * ratio * cross_next
        + ratio * ratio * curve_first
        + DAMP * (norm_next + 2.0 * ratio * mixed + ratio * ratio * norm)
    )
    step_second = norm_next / bottom
    along = step_first + step_second * ratio
    for out, first, second in pieces:
        out[...] = along * first + step_second * second


def hand_on(in_a, in_b, in_c, out_a, out_b, out_c, sems):
    copies = [
        pltpu.make_async_copy(source, target, sems.at[index])
        for index, (source, target) in enumerate(((in_a, out_a), (in_b, out_b), (in_c, out_c)))
    ]
    for copy in copies:
        copy.start()
    for copy in copies:
        copy.wait()


def local(tensor, observed, factor_a, factor_b, factor_c):
    sizes = (lax.axis_size("ia"), lax.axis_size("ja"), lax.axis_size("ka"))
    size_i, size_j, size_k = sizes
    count_a, count_b, count_c = size_j * size_k, size_i * size_k, size_i * size_j
    count = size_i * size_j * size_k
    depth, height, width = tensor.shape
    inverse = 32.0 / (width * size_j * depth * size_k)
    (own_a, own_b, own_c) = (factor_a.shape[1], factor_b.shape[1], factor_c.shape[1])
    columns = own_a * count_a
    cells = depth * height
    vmem = pltpu.VMEM
    operands = [
        pltpu.with_memory_space_constraint(operand, pltpu.HBM)
        for operand in (tensor, observed, factor_a.T, factor_b.T, factor_c.T)
    ]
    outs = pl.pallas_call(
        functools.partial(kernel, sizes, inverse),
        out_shape=(
            jax.ShapeDtypeStruct((own_a, height), F32),
            jax.ShapeDtypeStruct((own_b, width), F32),
            jax.ShapeDtypeStruct((own_c, depth), F32),
        ),
        in_specs=[pl.BlockSpec(memory_space=pltpu.HBM)] * 5,
        out_specs=(pl.BlockSpec(memory_space=pltpu.VMEM),) * 3,
        scratch_shapes=[
            vmem((depth, height, width), tensor.dtype),
            vmem((depth, height, width), observed.dtype),
            vmem((count_a, own_a, height), BF16),
            vmem((count_b, own_b, width), BF16),
            vmem((count_c, own_c, depth), BF16),
            vmem((columns, height), F32),
            vmem((columns, width), F32),
            vmem((columns, depth), F32),
            vmem((cells, columns), BF16),
            vmem((columns, cells), BF16),
            vmem((cells, width), F32),
            vmem((cells, width), F32),
            vmem((2, height, columns), BF16),
            vmem((2, columns, width), BF16),
            vmem((2, depth, columns), BF16),
            vmem((2, columns, width), BF16),
            vmem((2, depth, columns), BF16),
            vmem((2, count_a - 1, height, columns), BF16),
            vmem((2, size_k - 1, columns, width), BF16),
            vmem((2, size_j - 1, depth, columns), BF16),
            vmem((2, size_i - 1, columns, width), BF16),
            vmem((2, size_i - 1, depth, columns), BF16),
            vmem((height, columns), F32),
            vmem((columns, width), F32),
            vmem((depth, columns), F32),
            vmem((2, 1, 128), F32),
            vmem((2, count - 1, 1, 128), F32),
            pltpu.SemaphoreType.DMA((5,)),
            pltpu.SemaphoreType.DMA((3,)),
            pltpu.SemaphoreType.DMA((3,)),
            pltpu.SemaphoreType.DMA((2, 5)),
            pltpu.SemaphoreType.DMA((2, 5)),
            pltpu.SemaphoreType.DMA((2,)),
            pltpu.SemaphoreType.DMA((2,)),
        ],
        compiler_params=pltpu.CompilerParams(
            collective_id=0, has_side_effects=True, vmem_limit_bytes=VMEM_LIMIT
        ),
    )(*operands)
    outs = pl.pallas_call(
        hand_on,
        out_shape=tuple(jax.ShapeDtypeStruct(out.shape, F32) for out in outs),
        in_specs=[pl.BlockSpec(memory_space=pltpu.VMEM)] * 3,
        out_specs=(pl.BlockSpec(memory_space=pltpu.HBM),) * 3,
        scratch_shapes=[pltpu.SemaphoreType.DMA((3,))],
        compiler_params=pltpu.CompilerParams(vmem_limit_bytes=VMEM_LIMIT),
    )(*outs)
    return tuple(out.T for out in outs)


def solution(mesh):
    placed = (
        P("ka", "ia", "ja"),
        P("ka", "ia", "ja"),
        P("ia", ("ja", "ka")),
        P("ja", ("ia", "ka")),
        P("ka", ("ia", "ja")),
    )
    return jax.shard_map(
        local,
        mesh=mesh,
        in_specs=placed,
        out_specs=(P("ia", ("ja", "ka")), P("ja", ("ia", "ka")), P("ka", ("ia", "ja"))),
        check_vma=False,
    )
```

```python
import functools

import jax
import jax.numpy as jnp
from jax import lax
from jax.experimental import pallas as pl
from jax.experimental.pallas import tpu as pltpu
from jax.sharding import PartitionSpec as P

DAMP = 1.0
CHUNK_K = 8
UNROLL = 40
VMEM_LIMIT = 16 * 2**20
F32 = jnp.float32
BF16 = jnp.bfloat16


def each(count, body):
    if count <= UNROLL:
        for step in range(1, count):
            body(step)
    else:
        lax.fori_loop(1, count, lambda step, carry: (body(step), carry)[1], 0)


def mm(left, right):
    return jnp.dot(left, right, preferred_element_type=F32)


def total(array):
    rows, cols = array.shape
    folded = jnp.sum(array.reshape(rows // 8, 8, cols), axis=0) if rows > 8 else array
    return jnp.sum(jnp.sum(folded, axis=0, keepdims=True), axis=1, keepdims=True)


def kernel(
    sizes,
    inverse,
    tensor_hbm,
    observed_hbm,
    fa_hbm,
    fb_hbm,
    fc_hbm,
    out_a,
    out_b,
    out_c,
    tensor,
    observed,
    slot_a,
    slot_b,
    slot_c,
    flip_a,
    flip_b,
    flip_c,
    paired,
    paired_t,
    first_t,
    second_t,
    send_a,
    near_out_b,
    near_out_c,
    far_out_b,
    far_out_c,
    recv_a,
    near_b,
    near_c,
    far_b,
    far_c,
    grad_a,
    grad_b,
    grad_c,
    send_s,
    recv_s,
    load_sem,
    gather_send,
    gather_recv,
    part_send,
    part_recv,
    scal_send,
    scal_recv,
):
    size_i, size_j, size_k = sizes
    ia, ja, ka = lax.axis_index("ia"), lax.axis_index("ja"), lax.axis_index("ka")
    count_a, count_b, count_c = size_j * size_k, size_i * size_k, size_i * size_j
    count = size_i * size_j * size_k
    rank_a, rank_b, rank_c = ja * size_k + ka, ia * size_k + ka, ia * size_j + ja
    rank = rank_c * size_k + ka

    def peer_a(step):
        other = lax.rem(rank_a + step, count_a)
        return (ia, lax.div(other, size_k), lax.rem(other, size_k))

    def peer_b(step):
        other = lax.rem(rank_b + step, count_b)
        return (lax.div(other, size_k), ja, lax.rem(other, size_k))

    def peer_c(step):
        other = lax.rem(rank_c + step, count_c)
        return (lax.div(other, size_j), lax.rem(other, size_j), ka)

    def peer_all(step):
        other = lax.rem(rank + step, count)
        pair = lax.div(other, size_k)
        return (lax.div(pair, size_j), lax.rem(pair, size_j), lax.rem(other, size_k))

    def peer_i(step):
        return (lax.rem(ia + step, size_i), ja, ka)

    def peer_j(step):
        return (ia, lax.rem(ja + step, size_j), ka)

    def peer_k(step):
        return (ia, ja, lax.rem(ka + step, size_k))

    low = ia * 2 < size_i
    mirrored = jnp.where(low, size_i - 1 - ia, ia)

    def distant(turn):
        spot = turn + jnp.where(turn >= mirrored, 1, 0)
        return jnp.where(low, size_i - 1 - spot, spot)

    groups = ((count_a, peer_a), (count_b, peer_b), (count_c, peer_c))

    def send(source, target, send_sem, recv_sem, peer):
        pltpu.make_async_remote_copy(
            src_ref=source,
            dst_ref=target,
            send_sem=send_sem,
            recv_sem=recv_sem,
            device_id=peer,
            device_id_type=pl.DeviceIdType.MESH,
        ).start()

    def await_bytes(like, sem):
        pltpu.make_async_copy(like, like, sem).wait()

    barrier = pltpu.get_barrier_semaphore()

    def greet(peer):
        pl.semaphore_signal(barrier, inc=1, device_id=peer, device_id_type=pl.DeviceIdType.MESH)

    for step_i in range(1, size_i):
        for step_j in range(1, size_j):
            greet((lax.rem(ia + step_i, size_i), lax.rem(ja + step_j, size_j), ka))
        for step_k in range(size_k):
            greet((lax.rem(ia + step_i, size_i), ja, lax.rem(ka + step_k, size_k)))
    each(count_a, lambda step: greet(peer_a(step)))
    load_tensor = pltpu.make_async_copy(tensor_hbm, tensor, load_sem.at[0])
    load_observed = pltpu.make_async_copy(observed_hbm, observed, load_sem.at[1])
    shards = ((fa_hbm, slot_a, rank_a), (fb_hbm, slot_b, rank_b), (fc_hbm, slot_c, rank_c))
    own_loads = [
        pltpu.make_async_copy(shard, slots.at[own], load_sem.at[2 + index])
        for index, (shard, slots, own) in enumerate(shards)
    ]
    for load in own_loads:
        load.start()
    load_tensor.start()
    load_observed.start()

    for load in own_loads:
        load.wait()
    pl.semaphore_wait(barrier, (size_i - 1) * (size_j - 1 + size_k) + count_a - 1)

    for index in (2, 0, 1):
        _, slots, own = shards[index]
        members, peer = groups[index]

        def gather(step):
            send(slots.at[own], slots.at[own], gather_send.at[index], gather_recv.at[index], peer(step))

        each(members, gather)

    def assemble(index, slots, flip):
        members, width, _ = slots.shape
        await_bytes(slots.at[pl.ds(0, members - 1)], gather_recv.at[index])
        for step in range(members):
            flip[step * width : (step + 1) * width, :] = slots[step].astype(F32)
        return flip[...]

    wide_a = assemble(0, slot_a, flip_a).T
    wide_c = assemble(2, slot_c, flip_c).T
    depth, height, width = tensor.shape
    columns = wide_a.shape[1]
    rows = CHUNK_K * height
    chunks = depth // CHUNK_K

    def weight_of(chunk):
        cells = observed[chunk * CHUNK_K : (chunk + 1) * CHUNK_K].reshape(rows, width)
        return cells.astype(F32) * inverse

    def pick(wide, chunk):
        return wide[chunk * CHUNK_K : (chunk + 1) * CHUNK_K][:, None, :]

    for chunk in range(chunks):
        span = slice(chunk * rows, (chunk + 1) * rows)
        pairs = (pick(wide_c, chunk) * wide_a[None, :, :]).reshape(rows, columns).astype(BF16)
        paired[span, :] = pairs
        paired_t[:, span] = pairs.T
    turned_b = assemble(1, slot_b, flip_b)
    bt = turned_b.astype(BF16)
    full_b = turned_b.T.astype(BF16)
    load_tensor.wait()
    load_observed.wait()

    def spread(weighted, chunk, sums):
        mixture = mm(weighted, full_b).reshape(CHUNK_K, height, columns)
        sum_a = jnp.sum(mixture * pick(wide_c, chunk), axis=0)
        sum_c = jnp.sum(mixture * wide_a[None, :, :], axis=1)
        sum_b = mm(paired_t[:, chunk * rows : (chunk + 1) * rows], weighted)
        if sums is None:
            return [sum_a, sum_b, [sum_c]]
        return [sums[0] + sum_a, sums[1] + sum_b, sums[2] + [sum_c]]

    def fold(array):
        return jnp.sum(array.reshape(rows // 8, 8, width), axis=0)

    hops = (
        (send_a, recv_a, count_a, peer_a),
        (near_out_b, near_b, size_k, peer_k),
        (near_out_c, near_c, size_j, peer_j),
        (far_out_b, far_b, size_i, peer_i),
        (far_out_c, far_c, size_i, peer_i),
    )

    def post(turn, index, value):
        outbox, inbox, members, peer = hops[index]
        outbox[turn] = value.astype(BF16)
        if index >= 3:
            for order in range(size_i - 1):
                target = distant(order)
                send(
                    outbox.at[turn],
                    inbox.at[turn, lax.rem(target - ia + size_i, size_i) - 1],
                    part_send.at[turn, index],
                    part_recv.at[turn, index],
                    (target, ja, ka),
                )
            return

        def one(step):
            send(
                outbox.at[turn],
                inbox.at[turn, step - 1],
                part_send.at[turn, index],
                part_recv.at[turn, index],
                peer(step),
            )

        each(members, one)

    def collect(turn, index, own):
        inbox = hops[index][1]
        await_bytes(inbox.at[turn], part_recv.at[turn, index])
        for step in range(inbox.shape[1]):
            own = own + inbox[turn, step].astype(F32)
        return own

    def share(turn, sums):
        sum_a, sum_b, sum_c = sums[0], sums[1], jnp.concatenate(sums[2], axis=0)
        post(turn, 1, sum_b)
        post(turn, 2, sum_c)
        return sum_a, sum_b, sum_c

    def settle_ac(turn, own):
        sum_a, sum_b, sum_c = own
        sum_c = collect(turn, 2, sum_c)
        post(turn, 4, sum_c)
        sum_b = collect(turn, 1, sum_b)
        post(turn, 3, sum_b)
        post(turn, 0, sum_a)
        sum_a = collect(turn, 0, sum_a)
        sum_c = collect(turn, 4, sum_c)
        return sum_a, sum_b, sum_c

    def share_scalars(turn, values):
        lane = lax.broadcasted_iota(jnp.int32, (1, 128), 1)
        row = jnp.zeros((1, 128), F32)
        for index, value in enumerate(values):
            row = jnp.where(lane == index, value, row)
        send_s[turn] = row

        def post(step):
            send(
                send_s.at[turn],
                recv_s.at[turn, step - 1],
                scal_send.at[turn],
                scal_recv.at[turn],
                peer_all(step),
            )

        each(count, post)
        return row

    def collect_scalars(turn, row, number):
        await_bytes(recv_s.at[turn], scal_recv.at[turn])
        row = row + jnp.sum(recv_s[turn], axis=0)
        return [row[:, index : index + 1] for index in range(number)]

    sums = None
    for chunk in range(chunks):
        span = slice(chunk * rows, (chunk + 1) * rows)
        values = tensor[chunk * CHUNK_K : (chunk + 1) * CHUNK_K].reshape(rows, width).astype(F32)
        errors = (weight_of(chunk) * (values - mm(paired[span, :], bt))).astype(BF16)
        sums = spread(errors, chunk, sums)
    own = share(0, sums)
    shares = (1.0 / count_a, 1.0 / count_b, 1.0 / count_c)

    def inner(first, second, axes):
        return sum(total(first[axis] * second[axis]) * shares[axis] for axis in axes)

    def span_of(chunk):
        return slice(chunk * rows, (chunk + 1) * rows)

    def sideways_of(result, hat_a, hat_c):
        for chunk in range(chunks):
            mixed_a = pick(hat_c, chunk) * wide_a[None, :, :]
            mixed_c = pick(wide_c, chunk) * hat_a[None, :, :]
            result[span_of(chunk), :] = mm((mixed_a + mixed_c).reshape(rows, columns).astype(BF16), bt)

    def wide_hat(array):
        return array.astype(BF16).astype(F32)

    sum_a, sum_b, sum_c = settle_ac(0, own)
    grad_a[...] = sum_a
    grad_c[...] = sum_c
    sideways_of(first_t, wide_hat(sum_a), wide_hat(sum_c))
    sum_b = collect(0, 3, sum_b)
    grad_b[...] = sum_b

    hat_b = sum_b.astype(BF16)
    sums = None
    curve = jnp.zeros((8, width), F32)
    for chunk in range(chunks):
        tangent = first_t[span_of(chunk), :] + mm(paired[span_of(chunk), :], hat_b)
        first_t[span_of(chunk), :] = tangent
        weighted = weight_of(chunk) * tangent
        curve = curve + fold(weighted * tangent)
        sums = spread(weighted.astype(BF16), chunk, sums)
    own = share(1, sums)
    gradient = (grad_a[...], grad_b[...], grad_c[...])
    row = share_scalars(0, (inner(gradient, gradient, (0, 1, 2)), total(curve)))
    sum_a, sum_b, sum_c = settle_ac(1, own)
    norm, curve_first = collect_scalars(0, row, 2)
    step_first = norm / (curve_first + DAMP * norm)
    gradient = (grad_a[...], grad_b[...], grad_c[...])

    def residual_of(axis, part):
        return gradient[axis] - step_first * (part + DAMP * gradient[axis])

    rest_a, rest_c = residual_of(0, sum_a), residual_of(2, sum_c)
    sideways_of(second_t, wide_hat(rest_a), wide_hat(rest_c))
    residual = (rest_a, None, rest_c)
    norm_next = inner(residual, residual, (0, 2))
    mixed = inner(residual, gradient, (0, 2))
    residual = (rest_a, residual_of(1, collect(1, 3, sum_b)), rest_c)

    hat_b = residual[1].astype(BF16)
    curve = jnp.zeros((8, width), F32)
    cross = jnp.zeros((8, width), F32)
    for chunk in range(chunks):
        tangent = second_t[span_of(chunk), :] + mm(paired[span_of(chunk), :], hat_b)
        weighted = weight_of(chunk) * tangent
        curve = curve + fold(weighted * tangent)
        cross = cross + fold(weighted * first_t[span_of(chunk), :])
    norm_next = norm_next + inner(residual, residual, (1,))
    mixed = mixed + inner(residual, gradient, (1,))
    row = share_scalars(1, (norm_next, mixed, total(curve), total(cross)))

    def owned(flip, turned, own_rank, width_own):
        flip[...] = turned
        start = own_rank * width_own
        if width_own % 8 == 0:
            start = pl.multiple_of(start, 8)
        return flip[pl.ds(start, width_own), :]

    pieces = []
    for out, flip, own_rank, axis, turn in (
        (out_a, flip_a, rank_a, 0, True),
        (out_b, flip_b, rank_b, 1, False),
        (out_c, flip_c, rank_c, 2, True),
    ):
        width_own = out.shape[0]
        first = gradient[axis].T if turn else gradient[axis]
        second = residual[axis].T if turn else residual[axis]
        pieces.append(
            (out, owned(flip, first, own_rank, width_own), owned(flip, second, own_rank, width_own))
        )
    for sem_index, (like, members) in enumerate(
        ((slot_a, count_a), (slot_b, count_b), (slot_c, count_c))
    ):
        await_bytes(like.at[pl.ds(0, members - 1)], gather_send.at[sem_index])
    for turn in range(2):
        for index in range(5):
            await_bytes(hops[index][1].at[turn], part_send.at[turn, index])
        await_bytes(recv_s.at[turn], scal_send.at[turn])
    norm_next, mixed, curve_next, cross_next = collect_scalars(1, row, 4)
    ratio = norm_next / norm
    bottom = (
        curve_next
        + 2.0 * ratio * cross_next
        + ratio * ratio * curve_first
        + DAMP * (norm_next + 2.0 * ratio * mixed + ratio * ratio * norm)
    )
    step_second = norm_next / bottom
    along = step_first + step_second * ratio
    for out, first, second in pieces:
        out[...] = along * first + step_second * second


def hand_on(in_a, in_b, in_c, out_a, out_b, out_c, sems):
    copies = [
        pltpu.make_async_copy(source, target, sems.at[index])
        for index, (source, target) in enumerate(((in_a, out_a), (in_b, out_b), (in_c, out_c)))
    ]
    for copy in copies:
        copy.start()
    for copy in copies:
        copy.wait()


def local(tensor, observed, factor_a, factor_b, factor_c):
    sizes = (lax.axis_size("ia"), lax.axis_size("ja"), lax.axis_size("ka"))
    size_i, size_j, size_k = sizes
    count_a, count_b, count_c = size_j * size_k, size_i * size_k, size_i * size_j
    count = size_i * size_j * size_k
    depth, height, width = tensor.shape
    inverse = 32.0 / (width * size_j * depth * size_k)
    (own_a, own_b, own_c) = (factor_a.shape[1], factor_b.shape[1], factor_c.shape[1])
    columns = own_a * count_a
    cells = depth * height
    vmem = pltpu.VMEM
    operands = [
        pltpu.with_memory_space_constraint(operand, pltpu.HBM)
        for operand in (tensor, observed, factor_a.T, factor_b.T, factor_c.T)
    ]
    outs = pl.pallas_call(
        functools.partial(kernel, sizes, inverse),
        out_shape=(
            jax.ShapeDtypeStruct((own_a, height), F32),
            jax.ShapeDtypeStruct((own_b, width), F32),
            jax.ShapeDtypeStruct((own_c, depth), F32),
        ),
        in_specs=[pl.BlockSpec(memory_space=pltpu.HBM)] * 5,
        out_specs=(pl.BlockSpec(memory_space=pltpu.VMEM),) * 3,
        scratch_shapes=[
            vmem((depth, height, width), tensor.dtype),
            vmem((depth, height, width), observed.dtype),
            vmem((count_a, own_a, height), BF16),
            vmem((count_b, own_b, width), BF16),
            vmem((count_c, own_c, depth), BF16),
            vmem((columns, height), F32),
            vmem((columns, width), F32),
            vmem((columns, depth), F32),
            vmem((cells, columns), BF16),
            vmem((columns, cells), BF16),
            vmem((cells, width), F32),
            vmem((cells, width), F32),
            vmem((2, height, columns), BF16),
            vmem((2, columns, width), BF16),
            vmem((2, depth, columns), BF16),
            vmem((2, columns, width), BF16),
            vmem((2, depth, columns), BF16),
            vmem((2, count_a - 1, height, columns), BF16),
            vmem((2, size_k - 1, columns, width), BF16),
            vmem((2, size_j - 1, depth, columns), BF16),
            vmem((2, size_i - 1, columns, width), BF16),
            vmem((2, size_i - 1, depth, columns), BF16),
            vmem((height, columns), F32),
            vmem((columns, width), F32),
            vmem((depth, columns), F32),
            vmem((2, 1, 128), F32),
            vmem((2, count - 1, 1, 128), F32),
            pltpu.SemaphoreType.DMA((5,)),
            pltpu.SemaphoreType.DMA((3,)),
            pltpu.SemaphoreType.DMA((3,)),
            pltpu.SemaphoreType.DMA((2, 5)),
            pltpu.SemaphoreType.DMA((2, 5)),
            pltpu.SemaphoreType.DMA((2,)),
            pltpu.SemaphoreType.DMA((2,)),
        ],
        compiler_params=pltpu.CompilerParams(
            collective_id=0, has_side_effects=True, vmem_limit_bytes=VMEM_LIMIT
        ),
    )(*operands)
    outs = pl.pallas_call(
        hand_on,
        out_shape=tuple(jax.ShapeDtypeStruct(out.shape, F32) for out in outs),
        in_specs=[pl.BlockSpec(memory_space=pltpu.VMEM)] * 3,
        out_specs=(pl.BlockSpec(memory_space=pltpu.HBM),) * 3,
        scratch_shapes=[pltpu.SemaphoreType.DMA((3,))],
        compiler_params=pltpu.CompilerParams(vmem_limit_bytes=VMEM_LIMIT),
    )(*outs)
    return tuple(out.T for out in outs)


def solution(mesh):
    placed = (
        P("ka", "ia", "ja"),
        P("ka", "ia", "ja"),
        P("ia", ("ja", "ka")),
        P("ja", ("ia", "ka")),
        P("ka", ("ia", "ja")),
    )
    return jax.shard_map(
        local,
        mesh=mesh,
        in_specs=placed,
        out_specs=(P("ia", ("ja", "ka")), P("ja", ("ia", "ka")), P("ka", ("ia", "ja"))),
        check_vma=False,
    )
```
